32 devices in a mesh: feed: 8 (over z, x), tm: 4 (over y, core).
Axes of the slice: x: 2, y: 2, z: 4, core: 2. Of those that a mesh axis runs over, the one named last changes fastest.
Arguments:
- voltages: bfloat16 [2048, 131072], P('feed', 'tm'), may hold values from -6 to 6
- feed_slot: int32 [2048], replicated, may hold values from 0 to 2047, each once
- channel_flags: int32 [1024], replicated, may hold values from 0 to 1, as said below
Outputs:
- beam_power: float32 [96, 16, 1024], P(('feed', 'tm'))
The draws below stay inside these ranges and needn't reach their ends.
Inputs may be any that keep to these rules, and one draw needn't show every extreme that they name: `channel_flags`: exactly 96 entries are 1. `feed_slot`: each slot is named by exactly one input.
All inputs are finite; a program needn't handle non-finite values.
Results may differ from the reference program's by a relative error of at most 0.01.
Values may be sent and summed in bfloat16 or wider, within the bound.
A program may use at most 128 MiB of HBM per device.

```python
import math
import jax
import jax.numpy as jnp
from jax import lax

CHANNELS = 1024
TAPS = 4
CYL = 4
NS = 256
UPCH = 16
FRAME = 2048
INPUTS = 2048
FR_DEV = 16
IN_DEV = 256
LIVE = 96
N_TM = 4


def draw_channel_flags(key, part):
    shuffled = jax.random.permutation(jax.random.fold_in(key, 11), CHANNELS)
    return (shuffled < LIVE).astype(jnp.int32)


def shard_levels(rng, shape, split, least, top_value):
    def one(position, parts):
        heights = jax.random.uniform(jax.random.fold_in(jax.random.fold_in(rng, 6), position), (parts,), jnp.float32, least / len(split), top_value / len(split))
        return jnp.repeat(jnp.exp(heights), shape[position] // parts).reshape((-1,) + (1,) * (len(shape) - position - 1))

    level = one(*split[0])
    for cut in split[1:]:
        level = level * one(*cut)
    return level


def normal_values(own_key, extent, width, reach, shards=(), kind=jnp.bfloat16):
    gain = shard_levels(own_key, extent, shards, -0.22, 0.18) if shards else 1.0
    entries = jax.random.normal(own_key, extent, jnp.float32) * width * gain
    return jnp.minimum(jnp.maximum(entries, -reach), reach).astype(kind)


def setup_inputs(seed: int = 0) -> dict:
    keys = jax.random.split(jax.random.key(seed), 4)
    return {
        "voltages": normal_values(keys[0], (INPUTS, N_TM * FR_DEV * FRAME), 1.0, 6.0, ((0, 8), (1, 4))),
        "feed_slot": jax.random.permutation(keys[1], INPUTS).astype(jnp.int32),
        "channel_flags": draw_channel_flags(jax.random.fold_in(keys[3], 71), 0),
    }


def pfb_window():
    length = TAPS * 2 * CHANNELS
    sample = jnp.arange(length, dtype=jnp.float32)
    offset = (sample - length / 2 + 0.5) / (2 * CHANNELS)
    taper = 0.5 - 0.5 * jnp.cos(2.0 * jnp.pi * (sample + 0.5) / length)
    return (jnp.sinc(offset) * taper).reshape(TAPS, 2 * CHANNELS)

def phase_pair(modulus, first, second, scale):
    product = jnp.arange(first, dtype=jnp.int32)[:, None] * jnp.arange(second, dtype=jnp.int32)[None, :] % modulus
    angle = product.astype(jnp.float32) * (2.0 * jnp.pi / modulus)
    return (jnp.cos(angle) * scale, jnp.sin(angle) * scale)

def channel_table():
    cosine, sine = phase_pair(2 * CHANNELS, CHANNELS, 2 * CHANNELS, 1.0 / math.sqrt(2 * CHANNELS))
    return jnp.stack([cosine, -sine]).astype(jnp.bfloat16)

def grid_table():
    cosine, sine = phase_pair(NS, NS, NS, 1.0 / math.sqrt(NS))
    cosine = cosine.astype(jnp.bfloat16)
    sine = sine.astype(jnp.bfloat16)
    return jnp.stack([jnp.stack([cosine, -sine], axis=1), jnp.stack([sine, cosine], axis=1)])

def pfb_filter(extended, n_frames):
    window = pfb_window()
    summed = jnp.zeros((extended.shape[0], n_frames, extended.shape[2]), jnp.float32)
    for tap_index in range(TAPS):
        summed = summed + window[tap_index] * extended[:, tap_index:tap_index + n_frames].astype(jnp.float32)
    return summed.astype(jnp.bfloat16)

def beamform(spectra, inverse):
    highest = lax.Precision.HIGHEST
    chans, frames = (spectra.shape[0], spectra.shape[1])
    cells = jnp.take(spectra, inverse, axis=3).reshape(chans, frames, 2, 2, CYL, NS)
    ns_out = jnp.einsum('cfrpym,rmqn->cfpyqn', cells.astype(jnp.float32), grid_table().astype(jnp.float32), precision=highest)
    real_part = ns_out[:, :, :, :, 0]
    imag_part = ns_out[:, :, :, :, 1]
    ew_cos, ew_sin = phase_pair(CYL, CYL, CYL, 1.0 / math.sqrt(CYL))
    beam_re = jnp.einsum('cfpyn,ye->cfpen', real_part, ew_cos, precision=highest) + jnp.einsum('cfpyn,ye->cfpen', imag_part, ew_sin, precision=highest)
    beam_im = jnp.einsum('cfpyn,ye->cfpen', imag_part, ew_cos, precision=highest) - jnp.einsum('cfpyn,ye->cfpen', real_part, ew_sin, precision=highest)
    return jnp.stack([beam_re, beam_im], axis=2).astype(jnp.bfloat16)

def block_power(beams, blocks):
    highest = lax.Precision.HIGHEST
    chans = beams.shape[0]
    shaped = beams.reshape(chans, blocks, UPCH, 2, 2, CYL, NS).astype(jnp.float32)
    beam_re = shaped[:, :, :, 0]
    beam_im = shaped[:, :, :, 1]
    up_cos, up_sin = phase_pair(UPCH, UPCH, UPCH, 1.0 / math.sqrt(UPCH))
    up_cos = up_cos.astype(jnp.bfloat16).astype(jnp.float32)
    up_sin = up_sin.astype(jnp.bfloat16).astype(jnp.float32)
    up_re = jnp.einsum('cbupen,uk->cbkpen', beam_re, up_cos, precision=highest) + jnp.einsum('cbupen,uk->cbkpen', beam_im, up_sin, precision=highest)
    up_im = jnp.einsum('cbupen,uk->cbkpen', beam_im, up_cos, precision=highest) - jnp.einsum('cbupen,uk->cbkpen', beam_re, up_sin, precision=highest)
    summed = lax.optimization_barrier(jnp.sum(up_re * up_re + up_im * up_im, axis=(1, 3)))
    return summed.reshape(chans, UPCH, CYL * NS)

def reference(voltages, feed_slot, channel_flags):
    frame_len = 2 * CHANNELS
    n_frames = voltages.shape[1] // frame_len
    live_idx = jnp.nonzero(channel_flags, size=LIVE)[0].astype(jnp.int32)
    coeffs = jnp.take(channel_table(), live_idx, axis=1).astype(jnp.float32)

    def spectra_of(row_block):
        padding = jnp.zeros((row_block.shape[0], (TAPS - 1) * frame_len), jnp.bfloat16)
        extended = jnp.concatenate([padding, row_block], axis=1).reshape(row_block.shape[0], n_frames + TAPS - 1, frame_len)
        filtered = pfb_filter(extended, n_frames)
        return jnp.einsum('rcs,ifs->cfri', coeffs, filtered.astype(jnp.float32), precision=lax.Precision.HIGHEST).astype(jnp.bfloat16)
    grouped = voltages.reshape(INPUTS // IN_DEV, IN_DEV, voltages.shape[1])
    spectra = lax.map(spectra_of, grouped)
    spectra = jnp.moveaxis(spectra, 0, 3).reshape(LIVE, n_frames, 2, INPUTS)
    inverse = jnp.argsort(feed_slot).astype(jnp.int32)

    def channel_power(one_channel):
        beams = beamform(one_channel[None], inverse)
        return block_power(beams, n_frames // UPCH)[0]
    power_sum = lax.map(channel_power, spectra)
    return power_sum / (2.0 * (n_frames // UPCH))
```

```python
import math

import functools

import jax
import jax.numpy as jnp
import numpy as np
from jax import lax
from jax.experimental import pallas as pl
from jax.experimental.pallas import tpu as pltpu
from jax.sharding import PartitionSpec as P

CHANNELS = 1024
TAPS = 4
CYL = 4
NS = 256
UPCH = 16
LIVE_DEV = 3


def passed_along(block, axis, distance):
    devices = range(lax.axis_size(axis))
    route = [(i - distance, i) for i in devices if i - distance in devices]
    return lax.ppermute(block, axis, route)


def pfb_window():
    length = TAPS * 2 * CHANNELS
    sample = jnp.arange(length, dtype=jnp.float32)
    offset = (sample - length / 2 + 0.5) / (2 * CHANNELS)
    taper = 0.5 - 0.5 * jnp.cos(2.0 * jnp.pi * (sample + 0.5) / length)
    return (jnp.sinc(offset) * taper).reshape(TAPS, 2 * CHANNELS)


def phase_pair(modulus, first, second, scale):
    product = first[:, None] * second[None, :] % modulus
    angle = product.astype(jnp.float32) * (2.0 * jnp.pi / modulus)
    return (jnp.cos(angle) * scale, jnp.sin(angle) * scale)


def grid_table():
    index = jnp.arange(NS, dtype=jnp.int32)
    cosine, sine = phase_pair(NS, index, index, 1.0 / math.sqrt(NS))
    cosine = cosine.astype(jnp.bfloat16)
    sine = sine.astype(jnp.bfloat16)
    return cosine, sine


def live_channels(flags, count):
    k = jnp.arange(flags.shape[0], dtype=jnp.int32)
    seen = jnp.sum(jnp.where(k[None, :] <= k[:, None], flags[None, :], 0), axis=1)
    j = jnp.arange(count, dtype=jnp.int32)
    return jnp.sum((seen[None, :] <= j[:, None]).astype(jnp.int32), axis=1)


def pfb_filter(voltages, n_frames, window):
    inputs = voltages.shape[0]
    frames = voltages.reshape(inputs, n_frames, 2 * CHANNELS).astype(jnp.float32)
    padded = jnp.pad(frames, ((0, 0), (TAPS - 1, TAPS - 1), (0, 0)))
    total = n_frames + TAPS - 1
    summed = 0.0
    for tap in range(TAPS):
        summed = summed + window[tap] * padded[:, tap : tap + total]
    return summed.astype(jnp.bfloat16)


def local_plain(voltages, feed_slot, channel_flags):
    n_frames = voltages.shape[1] // (2 * CHANNELS)
    n_time = lax.axis_size("tm")
    n_feed = lax.axis_size("feed")
    inputs = voltages.shape[0]
    live_count = LIVE_DEV * n_feed * n_time
    chans = LIVE_DEV * n_time
    live = live_channels(channel_flags, live_count)
    cosine, sine = phase_pair(
        2 * CHANNELS, live, jnp.arange(2 * CHANNELS, dtype=jnp.int32), 1.0 / math.sqrt(2 * CHANNELS)
    )
    coeffs = jnp.stack([cosine, -sine]).astype(jnp.bfloat16)
    filtered = pfb_filter(voltages, n_frames, pfb_window())
    spectra = jnp.einsum("rcs,ifs->rcfi", coeffs, filtered, preferred_element_type=jnp.float32)
    earlier = passed_along(spectra[:, :, n_frames:].astype(jnp.bfloat16), "tm", 1)
    spectra = spectra[:, :, :n_frames]
    spectra = jnp.concatenate(
        [spectra[:, :, : TAPS - 1] + earlier.astype(jnp.float32), spectra[:, :, TAPS - 1 :]], axis=2
    ).astype(jnp.bfloat16)
    turned = lax.all_to_all(
        spectra.reshape(2, n_feed, chans, n_frames, inputs), "feed", split_axis=1, concat_axis=1, tiled=True
    )
    slots = feed_slot.reshape(n_feed, inputs)
    onehot = (slots[:, :, None] == jnp.arange(n_feed * inputs, dtype=jnp.int32)).astype(jnp.bfloat16)
    cells = jnp.einsum(
        "rscfi,sin->rcfn", turned, onehot, preferred_element_type=jnp.float32
    ).astype(jnp.bfloat16)
    cells = cells.reshape(2, chans, n_frames, 2 * CYL, NS)
    cosine, sine = grid_table()
    table = jnp.stack([jnp.stack([cosine, -sine], axis=1), jnp.stack([sine, cosine], axis=1)])
    ns_out = jnp.einsum("rcfgm,rmqn->qcfgn", cells, table, preferred_element_type=jnp.float32)
    z = ns_out.reshape(2, chans, n_frames, 2, CYL, NS)
    re, im = z[0], z[1]
    r = [re[:, :, :, y] for y in range(CYL)]
    i = [im[:, :, :, y] for y in range(CYL)]
    t0r, t1r, t2r, t3r = r[0] + r[2], r[0] - r[2], r[1] + r[3], r[1] - r[3]
    t0i, t1i, t2i, t3i = i[0] + i[2], i[0] - i[2], i[1] + i[3], i[1] - i[3]
    beam_re = jnp.stack([t0r + t2r, t1r + t3i, t0r - t2r, t1r - t3i], axis=3)
    beam_im = jnp.stack([t0i + t2i, t1i - t3r, t0i - t2i, t1i + t3r], axis=3)
    beams = (jnp.stack([beam_re, beam_im]) * 0.5).astype(jnp.bfloat16)
    blocks = n_frames // UPCH
    beams = beams.reshape(2, chans, blocks, UPCH, 2, CYL * NS)
    index = jnp.arange(UPCH, dtype=jnp.int32)
    up_cos, up_sin = phase_pair(UPCH, index, index, 1.0 / math.sqrt(UPCH))
    up_cos = up_cos.astype(jnp.bfloat16)
    up_sin = up_sin.astype(jnp.bfloat16)
    up_table = jnp.stack([jnp.stack([up_cos, -up_sin], axis=1), jnp.stack([up_sin, up_cos], axis=1)])
    up = jnp.einsum("qcbupn,quvk->vcbkpn", beams, up_table, preferred_element_type=jnp.float32)
    power = jnp.sum(up * up, axis=(0, 2, 4)) * (1.0 / (2.0 * n_time * blocks))
    parts = lax.all_to_all(
        power.astype(jnp.bfloat16).reshape(n_time, LIVE_DEV, UPCH, CYL * NS), "tm", split_axis=0, concat_axis=0, tiled=True
    )
    return jnp.sum(parts.astype(jnp.float32), axis=0)


MESH = pl.DeviceIdType.MESH
NT = (((1,), (1,)), ((), ()))
BF = jnp.bfloat16
F32 = jnp.float32


def flip(index, bits, top):
    total = 0
    while top:
        total = total + top * lax.rem(lax.rem(index // top, 2) + lax.rem(bits // top, 2), 2)
        top //= 2
    return total


def quarter_wave():
    half = math.pi / 2
    return [(-1.0) ** k * half ** (2 * k + 1) / math.factorial(2 * k + 1) for k in range(6)]


def turn_cos(index, period):
    quarter = period // 4
    x = (jnp.abs(index - 2 * quarter) - quarter).astype(F32) * (1.0 / quarter)
    y = x * x
    series = quarter_wave()
    value = series[-1]
    for term in series[-2::-1]:
        value = value * y + term
    return value * x


def fused_kernel(
    n_feed, n_time, n_frames, scale,
    volt, flags_in, window_in, slots_in, table_in, ua_in, pa_in, pb_in, out,
    vp, flags, window, slots, table, ua, pa, pb, result,
    coeffs, filt, spec, hist_out, hist_in, send_a, recv_a, send_b, recv_b,
    onehot, ns, acc, stacked,
    load_sem, in_sem, out_sem, own_sem, hist_sem, send_sem, recv_sem, bsend_sem, brecv_sem,
):
    me = lax.axis_index("feed")
    tm = lax.axis_index("tm")
    frame = 2 * CHANNELS
    past = TAPS - 1
    quads = n_frames // 4
    inputs = volt.shape[0]
    total = n_feed * inputs
    dests = n_feed * n_time
    rows_a = 4 * dests

    def load(f):
        return pltpu.make_async_copy(
            volt.at[:, pl.ds(f * frame, frame)], vp.at[f], load_sem.at[f]
        )

    tables = [
        (flags_in, flags), (window_in, window), (pa_in, pa), (slots_in, slots),
        (pb_in, pb), (ua_in, ua), (table_in, table),
    ]

    def fetch(k):
        return pltpu.make_async_copy(tables[k][0], tables[k][1], in_sem.at[k])

    fetch(0).start()
    fetch(1).start()
    for f in range(1, 8):
        load(f).start()
    barrier = pltpu.get_barrier_semaphore()

    def greet(i, _):
        pl.semaphore_signal(
            barrier, inc=1, device_id={"feed": flip(me, i // n_time, n_feed // 2), "tm": flip(tm, lax.rem(i, n_time), n_time // 2)},
            device_id_type=MESH,
        )
        return 0

    lax.fori_loop(1, dests, greet, 0)
    for f in list(range(8, n_frames)) + [0]:
        load(f).start()
    for k in range(2, len(tables)):
        fetch(k).start()

    def send_copy(q, i):
        m, t = i // n_time, lax.rem(i, n_time)
        to, tt = flip(me, m, n_feed // 2), flip(tm, t, n_time // 2)
        return pltpu.make_async_remote_copy(
            src_ref=send_a.at[q, to * n_time + tt],
            dst_ref=recv_a.at[pl.ds(pl.multiple_of((tm * quads + q) * 16, 16), 16), pl.ds(pl.multiple_of(me * inputs, 256), inputs)],
            send_sem=send_sem.at[q, i], recv_sem=recv_sem.at[q, i],
            device_id={"feed": to, "tm": tt}, device_id_type=MESH,
        )

    def arrival(q, i):
        m, t = i // n_time, lax.rem(i, n_time)
        to, tt = flip(me, m, n_feed // 2), flip(tm, t, n_time // 2)
        return pltpu.make_async_remote_copy(
            src_ref=send_a.at[q, to * n_time + tt],
            dst_ref=recv_a.at[pl.ds(pl.multiple_of((tt * quads + q) * 16, 16), 16), pl.ds(pl.multiple_of(to * inputs, 256), inputs)],
            send_sem=send_sem.at[q, i], recv_sem=recv_sem.at[q, i],
            device_id={"feed": to, "tm": tt}, device_id_type=MESH,
        )

    def own_copy(q):
        return pltpu.make_async_copy(
            send_a.at[q, me * n_time + tm],
            recv_a.at[pl.ds(pl.multiple_of((tm * quads + q) * 16, 16), 16), pl.ds(pl.multiple_of(me * inputs, 256), inputs)],
            own_sem.at[q],
        )

    def bsend_copy(i):
        m, t = i // n_time, lax.rem(i, n_time)
        to, tt = flip(me, m, n_feed // 2), flip(tm, t, n_time // 2)
        return pltpu.make_async_remote_copy(
            src_ref=send_b.at[to * n_time + tt],
            dst_ref=recv_b.at[pl.ds(pl.multiple_of(tm * 32, 32), 32), pl.ds(pl.multiple_of(me * inputs, 256), inputs)],
            send_sem=bsend_sem.at[i], recv_sem=brecv_sem.at[i],
            device_id={"feed": to, "tm": tt}, device_id_type=MESH,
        )

    def barrival(i):
        m, t = i // n_time, lax.rem(i, n_time)
        to, tt = flip(me, m, n_feed // 2), flip(tm, t, n_time // 2)
        return pltpu.make_async_remote_copy(
            src_ref=send_b.at[to * n_time + tt],
            dst_ref=recv_b.at[pl.ds(pl.multiple_of(tt * 32, 32), 32), pl.ds(pl.multiple_of(to * inputs, 256), inputs)],
            send_sem=bsend_sem.at[i], recv_sem=brecv_sem.at[i],
            device_id={"feed": to, "tm": tt}, device_id_type=MESH,
        )

    def bown_copy():
        return pltpu.make_async_copy(
            send_b.at[me * n_time + tm],
            recv_b.at[pl.ds(pl.multiple_of(tm * 32, 32), 32), pl.ds(pl.multiple_of(me * inputs, 256), inputs)],
            own_sem.at[quads],
        )

    def each(first, last, body):
        def step(i, _):
            body(i)
            return 0

        lax.fori_loop(first, last, step, 0)

    def hist_copy(to):
        return pltpu.make_async_remote_copy(
            src_ref=hist_out, dst_ref=hist_in, send_sem=hist_sem.at[0], recv_sem=hist_sem.at[1],
            device_id={"tm": to}, device_id_type=MESH,
        )

    fetch(0).wait()
    kept = flags[...].astype(F32)
    lane = lax.broadcasted_iota(jnp.int32, (128, 128), 1)
    sub = lax.broadcasted_iota(jnp.int32, (128, 128), 0)
    upto = jnp.dot(kept, jnp.where(sub <= lane, 1.0, 0.0), preferred_element_type=F32)
    whole = jnp.dot(kept, jnp.ones((128, 128), F32), preferred_element_type=F32)
    seen, before = [], jnp.zeros((1, 128), F32)
    for a in range(CHANNELS // 128):
        seen.append(upto[a : a + 1] + before)
        before = before + whole[a : a + 1]
    block = 48
    norm = 1.0 / math.sqrt(frame)

    def coeff_rows(r, _):
        row = lax.broadcasted_iota(jnp.int32, (block, 128), 0) + r * block
        step = lax.broadcasted_iota(jnp.int32, (block, 128), 1)
        early = row < rows_a
        dest = jnp.where(early, lax.shift_right_logical(row, 2), lax.shift_right_logical(row - rows_a, 1))
        chan = dest * LIVE_DEV + jnp.where(early, lax.shift_right_logical(row, 1) & 1, 2)
        chan = chan.astype(F32)
        shift = (row & 1) * (frame // 4)
        count = jnp.zeros((block, 128), F32)
        for one in seen:
            count = count + jnp.where(one <= chan, 1.0, 0.0)
        live = jnp.sum(count, axis=1, keepdims=True).astype(jnp.int32)
        fine = live * step
        fine_cos = turn_cos(fine & (frame - 1), frame)
        fine_sin = turn_cos((fine + 3 * frame // 4) & (frame - 1), frame)
        coarse = live * ((step & 15) * 128) + shift + jnp.where(step >= 16, 3 * frame // 4, 0)
        coarse = turn_cos(coarse & (frame - 1), frame) * norm
        at = pl.ds(pl.multiple_of(r * block, 16), block)
        for k in range(frame // 128):
            value = coarse[:, k : k + 1] * fine_cos - coarse[:, 16 + k : 17 + k] * fine_sin
            coeffs[at, k * 128 : (k + 1) * 128] = value.astype(BF)
        return 0

    lax.fori_loop(0, coeffs.shape[0] // block, coeff_rows, 0)
    fetch(1).wait()

    def filtered(f, slot, taps):
        for k in range(frame // 128):
            lanes = slice(k * 128, (k + 1) * 128)
            terms = {}
            for t in taps:
                w = jnp.concatenate([window[t, :, lanes]] * (inputs // 16), axis=0)
                terms[t] = w * vp[f + t - past, :, lanes]
            ends = [terms[t] for t in (0, past) if t in terms]
            middle = [terms[t] for t in range(1, past) if t in terms]
            parts = [functools.reduce(jnp.add, group) for group in (ends, middle) if group]
            filt[slot, :, lanes] = functools.reduce(jnp.add, parts)

    def spectra(slot):
        return lax.dot_general(coeffs[...], filt[slot], NT, preferred_element_type=F32)

    every = tuple(range(TAPS))

    def run(frames, keep):
        filtered(frames[0][0], 0, frames[0][1])
        for k in range(len(frames)):
            if k + 1 < len(frames):
                filtered(frames[k + 1][0], (k + 1) % 2, frames[k + 1][1])
            keep(k, spectra(k % 2))

    def pack(q):
        for j in range(rows_a // 32):
            data = jnp.concatenate([spec[4 * q + k, 32 * j : 32 * j + 32, :] for k in range(4)], axis=0)
            moved = jnp.dot(pa[...], data, preferred_element_type=F32)
            send_a[q, 8 * j : 8 * j + 8] = moved.astype(BF).reshape(8, 16, inputs)

    def send_quad(q):
        each(dests // 2, dests, lambda i: send_copy(q, i).start())
        each(1, dests // 2, lambda i: send_copy(q, i).start())
        own_copy(q).start()

    def middle_quad(q, _):
        for k in range(4):
            load(4 * q + k).wait()

        def keep(k, value):
            spec[4 * q + k] = value.astype(BF)

        run([(4 * q + k, every) for k in range(4)], keep)
        pack(q)

        @pl.when(q == 1)
        def _():
            pl.semaphore_wait(barrier, dests - 1)

        send_quad(q)
        return 0

    for f in range(1, 4):
        load(f).wait()
    fetch(2).wait()
    lax.fori_loop(1, quads, middle_quad, 0)

    def keep_tail(k, value):
        hist_out[k] = value.astype(BF)

    run([(n_frames + k, tuple(range(past - k))) for k in range(past)], keep_tail)

    @pl.when(tm < n_time - 1)
    def _():
        hist_copy(lax.rem(tm + 1, n_time)).start()

    fetch(3).wait()
    which = lax.broadcasted_iota(jnp.int32, (inputs, inputs), 0)

    def ones(g, _):
        for s in range(n_feed):
            hit = which == slots[s] - g * inputs
            onehot[pl.ds(pl.multiple_of(g * inputs, 256), inputs), s * inputs : (s + 1) * inputs] = jnp.where(hit, 1.0, 0.0).astype(BF)
        return 0

    load(0).wait()

    @pl.when(tm > 0)
    def _():
        hist_copy(lax.rem(tm + n_time - 1, n_time)).wait_recv()

    @pl.when(tm == 0)
    def _():
        hist_in[...] = jnp.zeros_like(hist_in)

    def keep_first(k, value):
        if k < past:
            value = value + hist_in[k].astype(F32)
        spec[k] = value.astype(BF)

    run([(k, tuple(range(max(past - k, 0), TAPS))) for k in range(4)], keep_first)
    pack(0)
    send_quad(0)
    fetch(4).wait()
    for j in range(dests // 8):
        data = jnp.concatenate([spec[f, rows_a + 16 * j : rows_a + 16 * j + 16, :] for f in range(n_frames)], axis=0)
        moved = jnp.dot(pb[...], data, preferred_element_type=F32)
        send_b[8 * j : 8 * j + 8] = moved.astype(BF).reshape(8, 32, inputs)
    each(dests // 2, dests, lambda i: bsend_copy(i).start())
    each(1, dests // 2, lambda i: bsend_copy(i).start())
    bown_copy().start()

    lax.fori_loop(0, n_feed, ones, 0)
    fetch(5).wait()
    fetch(6).wait()

    def wait_quad(q, _):
        own_copy(q).wait()
        each(1, dests, lambda i: arrival(q, i).wait_recv())
        return 0

    lax.fori_loop(0, quads, wait_quad, 0)
    half = 4 * n_time * UPCH // 4

    def beam_a(g, _):
        at = pl.ds(pl.multiple_of(g * inputs, 256), inputs)
        cells = lax.dot_general(recv_a[...], onehot[at, :], NT, preferred_element_type=F32).astype(BF)
        up = jnp.dot(ua[...], cells, preferred_element_type=F32).astype(BF)
        both = jnp.concatenate([
            jnp.concatenate([up[0:half], up[2 * half : 3 * half]], axis=0),
            jnp.concatenate([up[half : 2 * half], up[3 * half :]], axis=0),
        ], axis=1)
        value = jnp.dot(both, table[...], preferred_element_type=F32)
        ns[0, pl.ds(pl.multiple_of(g * half, half), half)] = value[:half]
        ns[1, pl.ds(pl.multiple_of(g * half, half), half)] = value[half:]
        return 0

    lax.fori_loop(0, n_feed, beam_a, 0)

    def power(c, chan):
        for e0 in range(NS // 128):
            lanes = slice(e0 * 128, e0 * 128 + 128)
            more = slice(NS + e0 * 128, NS + e0 * 128 + 128)
            sums = [0.0] * CYL
            for p in range(2):
                z = []
                for y in range(CYL):
                    at = slice((p * CYL + y) * half, (p * CYL + y + 1) * half)
                    z.append((ns[c, at, lanes], ns[c, at, more]))
                (r0, i0), (r1, i1), (r2, i2), (r3, i3) = z
                t0r, t1r, t2r, t3r = r0 + r2, r0 - r2, r1 + r3, r1 - r3
                t0i, t1i, t2i, t3i = i0 + i2, i0 - i2, i1 + i3, i1 - i3
                re = [t0r + t2r, t1r + t3i, t0r - t2r, t1r - t3i]
                im = [t0i + t2i, t1i - t3r, t0i - t2i, t1i + t3r]
                for e in range(CYL):
                    sums[e] = sums[e] + re[e] * re[e] + im[e] * im[e]
            for e in range(CYL):
                parts = sums[e].reshape(n_time, UPCH, 128)
                value = parts[0]
                for t in range(1, n_time):
                    value = value + parts[t]
                result[chan, :, e * NS + e0 * 128 : e * NS + e0 * 128 + 128] = value * scale

    def out_copy(c):
        return pltpu.make_async_copy(result.at[c], out.at[c], out_sem.at[c])

    power(0, 0)
    power(1, 1)
    out_copy(0).start()
    out_copy(1).start()

    bown_copy().wait()
    each(1, dests // 2, lambda i: barrival(i).wait_recv())
    home = pl.multiple_of(me // (n_feed // 2) * (total // 2), 256)

    def near(g, _):
        at = pl.ds(pl.multiple_of(g * inputs, 256), inputs)
        near_cols = pl.ds(home, total // 2)
        acc[g] = lax.dot_general(recv_b[:, near_cols], onehot[at, near_cols], NT, preferred_element_type=F32)
        return 0

    lax.fori_loop(0, n_feed, near, 0)

    def source(m, _):
        each(m * n_time, (m + 1) * n_time, lambda i: barrival(i).wait_recv())
        cols = pl.ds(pl.multiple_of(flip(me, m, n_feed // 2) * inputs, 256), inputs)

        def add(g, _):
            at = pl.ds(pl.multiple_of(g * inputs, 256), inputs)
            acc[g] += lax.dot_general(recv_b[:, cols], onehot[at, cols], NT, preferred_element_type=F32)
            return 0

        lax.fori_loop(0, n_feed, add, 0)
        return 0

    lax.fori_loop(n_feed // 2, n_feed - 1, source, 0)
    last = n_feed - 1
    each(last * n_time, (last + 1) * n_time, lambda i: barrival(i).wait_recv())
    cols = pl.ds(pl.multiple_of(flip(me, last, n_feed // 2) * inputs, 256), inputs)
    for g in range(n_feed):
        got = lax.dot_general(recv_b[:, cols], onehot[g * inputs : (g + 1) * inputs, cols], NT, preferred_element_type=F32)
        got = (acc[g] + got).astype(BF).reshape(n_time, 2, UPCH, inputs)
        for part in range(2):
            stacked[g * half : (g + 1) * half, part * inputs : (part + 1) * inputs] = got[:, part].reshape(half, inputs)
    ns[0] = jnp.dot(stacked[...], table[...], preferred_element_type=F32)
    power(0, 2)
    out_copy(2).start()

    def drain(q, _):
        each(1, dests, lambda i: send_copy(q, i).wait_send())
        return 0

    lax.fori_loop(0, quads, drain, 0)
    each(1, dests, lambda i: bsend_copy(i).wait_send())

    @pl.when(tm < n_time - 1)
    def _():
        hist_copy(lax.rem(tm + 1, n_time)).wait_send()

    for c in range(LIVE_DEV):
        out_copy(c).wait()


def rounded_pair(modulus, first, second):
    angle = (first[:, None] * second[None, :] % modulus) * (2.0 * np.pi / modulus)
    scale = 1.0 / np.sqrt(modulus)
    return (
        (np.cos(angle) * scale).astype(np.float32).astype(BF),
        (np.sin(angle) * scale).astype(np.float32).astype(BF),
    )


def window_table():
    length = TAPS * 2 * CHANNELS
    sample = np.arange(length)
    offset = (sample - length / 2 + 0.5) / (2 * CHANNELS)
    taper = 0.5 - 0.5 * np.cos(2.0 * np.pi * (sample + 0.5) / length)
    return (np.sinc(offset) * taper).astype(np.float32).reshape(TAPS, 2 * CHANNELS)


def up_matrix(frames):
    c, s = rounded_pair(UPCH, np.arange(UPCH), np.arange(frames))
    c, s = c.astype(np.float32), s.astype(np.float32)
    return np.stack([np.stack([c, s], -1), np.stack([-s, c], -1)])


def row_tables(n_frames, n_time):
    up = up_matrix(n_frames)
    pa = np.einsum("da,fb,xc->dfxbac", np.eye(8), np.eye(4), np.eye(4)).reshape(128, 128)
    pb = np.einsum("da,vkfr->dvkfar", np.eye(8), up).reshape(8 * 2 * UPCH, n_frames * 16)
    ua = np.einsum("gc,tb,vkfr->gvtkbfcr", np.eye(2), np.eye(n_time), up)
    ua = ua.reshape(4 * n_time * UPCH, n_time * n_frames * 4)
    return [jnp.array(one.astype(np.float32).astype(BF)) for one in (ua, pa, pb)]


def local_fused(voltages, feed_slot, channel_flags):
    frame = 2 * CHANNELS
    inputs = voltages.shape[0]
    n_frames = voltages.shape[1] // frame
    n_time = lax.axis_size("tm")
    n_feed = lax.axis_size("feed")
    quads = n_frames // 4
    dests = n_feed * n_time
    rows = 2 * LIVE_DEV * dests
    total = n_feed * inputs
    index = np.arange(NS)
    c, d = rounded_pair(NS, index, index)
    table = jnp.array(np.concatenate([np.concatenate([c, -d], axis=1), np.concatenate([d, c], axis=1)], axis=0))
    ua, pa, pb = row_tables(n_frames, n_time)
    window = jnp.array(np.repeat(window_table().astype(BF)[:, None, :], 16, axis=1))
    operands = [
        voltages, channel_flags.reshape(CHANNELS // 128, 128), window, feed_slot.reshape(n_feed, 1, inputs),
        table, ua, pa, pb,
    ]
    dma = pltpu.SemaphoreType.DMA
    staged = [pltpu.VMEM(one.shape, one.dtype) for one in operands[1:]]
    half = n_time * UPCH
    return pl.pallas_call(
        functools.partial(fused_kernel, n_feed, n_time, n_frames, 0.25 / (2.0 * n_time)),
        out_shape=jax.ShapeDtypeStruct((LIVE_DEV, UPCH, CYL * NS), F32),
        in_specs=[pl.BlockSpec(memory_space=pl.ANY)] * len(operands),
        out_specs=pl.BlockSpec(memory_space=pl.ANY),
        scratch_shapes=[pltpu.VMEM((n_frames, inputs, frame), BF)] + staged + [
            pltpu.VMEM((LIVE_DEV, UPCH, CYL * NS), F32),
            pltpu.VMEM((rows, frame), BF),
            pltpu.VMEM((2, inputs, frame), BF),
            pltpu.VMEM((n_frames, rows, inputs), BF),
            pltpu.VMEM((TAPS - 1, rows, inputs), BF),
            pltpu.VMEM((TAPS - 1, rows, inputs), BF),
            pltpu.VMEM((quads, dests, 16, inputs), BF),
            pltpu.VMEM((n_time * quads * 16, total), BF),
            pltpu.VMEM((dests, 2 * UPCH, inputs), BF),
            pltpu.VMEM((n_time * 2 * UPCH, total), BF),
            pltpu.VMEM((total, total), BF),
            pltpu.VMEM((2, n_feed * half, 2 * NS), F32),
            pltpu.VMEM((n_feed, 2 * half, NS), F32),
            pltpu.VMEM((n_feed * half, 2 * NS), BF),
            dma((n_frames,)),
            dma((len(operands) - 1,)),
            dma((LIVE_DEV,)),
            dma((quads + 1,)),
            dma((2,)),
            dma((quads, dests)),
            dma((quads, dests)),
            dma((dests,)),
            dma((dests,)),
        ],
        compiler_params=pltpu.CompilerParams(
            collective_id=0, has_side_effects=True, vmem_limit_bytes=62 * 1024 * 1024
        ),
    )(*operands)


def local(voltages, feed_slot, channel_flags):
    fits = (
        voltages.shape[0] == NS
        and voltages.shape[1] == UPCH * 2 * CHANNELS
        and lax.axis_size("tm") == 4
        and lax.axis_size("feed") == 8
        and lax.axis_size("feed") * voltages.shape[0] == 2 * CYL * NS
    )
    return (local_fused if fits else local_plain)(voltages, feed_slot, channel_flags)


def solution(mesh):
    in_specs = (P("feed", "tm"), P(), P())
    out_specs = P(("feed", "tm"), None, None)
    return jax.shard_map(local, mesh=mesh, in_specs=in_specs, out_specs=out_specs, check_vma=False)
```
